128 devices in a mesh: row: 16 (over x, z), col: 8 (over y, core).
Axes of the slice: x: 4, y: 4, z: 4, core: 2. Of those that a mesh axis runs over, the one named last changes fastest.
Arguments:
- diag_one: float32 [512, 512], P('row'), as said below
- coupling: float32 [512, 512], P('row'), may hold values from -0.25 to 0.25
- diag_two: float32 [512, 512], P('row'), as said below
- off_one: float32 [32768, 512], P(('row', 'col')), may hold values from -2 to 2
- off_two: float32 [32768, 512], P(('row', 'col')), may hold values from -2 to 2
- targets: float32 [16384, 128, 128], P(('row', 'col')), may hold values from -6 to 6
- pattern: int32 [16384, 2], P(('row', 'col')), may hold values from 0 to 255, as said below
Outputs:
- lower_one: float32 [32768, 512], P(('row', 'col'))
- lower_two: float32 [32768, 512], P(('row', 'col'))
- updated: float32 [16384, 128, 128], P(('row', 'col'))
The draws below stay inside these ranges and needn't reach their ends.
Inputs may be any that keep to these rules, and one draw needn't show every extreme that they name: Rows of pattern come in groups of 128; group f belongs to grid position (r, c) = (f // 8, f % 8) of the row and col axes (sizes 16, 8). Its block rows i lie in r * 8 * 2 to (r + 1) * 8 * 2 - 1; its block columns j satisfy (j // 2) % 8 == c; always j <= i. Pairs may repeat. `diag_one`: Symmetric, diagonal entries 2.5, other entries of magnitude at most W^-0.5. `diag_two`: Symmetric, diagonal entries 6, other entries of magnitude at most W^-0.5.
All inputs are finite; a program needn't handle non-finite values.
Results may differ from the reference program's by a relative error of at most 0.00005.
Values sent between devices are 32-bit elements; how exact they have to be, the bound alone decides.
No kernel may reach another device: no remote copies, remote signals or barrier semaphores. Data moves between devices by JAX's collectives and lax.ppermute only.
A program may use at most 128 MiB of HBM per device.

```python
import jax
import jax.numpy as jnp
from jax import lax

W = 512
BLK = 128
BD = 2
KD = 128
NBLK = 256
M = 32768
KTOT = 16384
N_COL = 8


def symmetric_block(key, diag_value):
    scale = W ** (-0.5)
    raw = jax.random.uniform(key, (W, W), jnp.float32, minval=-scale, maxval=scale)
    sym = 0.5 * (raw + raw.T)
    identity = jnp.eye(W, dtype=jnp.float32)
    return sym * (1.0 - identity) + diag_value * identity


def draw_diag_one(key, part):
    return symmetric_block(jax.random.fold_in(key, 11), 2.5)


def draw_diag_two(key, part):
    return symmetric_block(jax.random.fold_in(key, 22), 6.0)


def draw_pattern(key, part):
    first_key = jax.random.fold_in(key, 31)
    second_key = jax.random.fold_in(key, 32)
    device = jnp.arange(KTOT, dtype=jnp.int32) // KD
    slot = jnp.arange(KTOT, dtype=jnp.int32) % KD
    grid_row = device // N_COL
    grid_col = device % N_COL
    local_col = jax.random.randint(first_key, (KTOT,), 0, (grid_row + 1) * BD, dtype=jnp.int32)
    local_col = jnp.where(slot == 0, 0, local_col)
    block_col = (local_col // BD * N_COL + grid_col) * BD + local_col % BD
    start = grid_row * N_COL * BD
    finish = start + N_COL * BD
    lowest = jnp.maximum(block_col, start)
    block_row = jax.random.randint(second_key, (KTOT,), lowest, finish, dtype=jnp.int32)
    block_row = jnp.where(slot == 0, finish - 1, block_row)
    return jnp.stack([block_row, block_col], axis=1).astype(jnp.int32)


def level_of(own_key, dims, pieces, least, largest):
    factor_of = 1.0
    for axis_at, parts in pieces:
        heights = jax.random.uniform(jax.random.fold_in(jax.random.fold_in(own_key, 6), axis_at), (parts,), jnp.float32, least / len(pieces), largest / len(pieces))
        factor_of = factor_of * jnp.repeat(jnp.exp(heights), dims[axis_at] // parts).reshape((-1,) + (1,) * (len(dims) - 1 - axis_at))
    return factor_of


def centred(own_key, dims, width, reach, split=(), held_as=jnp.bfloat16):
    array = jax.random.normal(own_key, dims, jnp.float32) * width
    if len(split) > 0:
        array = level_of(own_key, dims, split, -0.22, 0.18) * array
    return jnp.clip(array, min=-reach, max=reach).astype(held_as)


def setup_inputs(seed: int = 0) -> dict:
    key_list = jax.random.split(jax.random.key(seed), 8)
    diag_one = draw_diag_one(jax.random.fold_in(key_list[7], 71), 0)
    coupling = centred(key_list[1], (W, W), W ** -0.5, 0.25, ((0, 16),), jnp.float32)
    diag_two = draw_diag_two(jax.random.fold_in(key_list[7], 71), 0)
    off_one = centred(key_list[3], (M, W), 0.3333, 2.0, ((0, 128),), jnp.float32)
    off_two = centred(key_list[4], (M, W), 0.3333, 2.0, ((0, 128),), jnp.float32)
    targets = centred(key_list[5], (KTOT, BLK, BLK), 1.0, 6.0, ((0, 128),), jnp.float32)
    pattern = draw_pattern(jax.random.fold_in(key_list[7], 71), 0)
    return dict(diag_one=diag_one, coupling=coupling, diag_two=diag_two, off_one=off_one, off_two=off_two, targets=targets, pattern=pattern)


def right_solve(chol, rows):
    return lax.linalg.triangular_solve(chol, rows, left_side=False, lower=True, transpose_a=True)

def reference(diag_one, coupling, diag_two, off_one, off_two, targets, pattern):
    highest = lax.Precision.HIGHEST
    chol_one = jnp.linalg.cholesky(diag_one)
    lower_coupling = right_solve(chol_one, coupling)
    lower_one = right_solve(chol_one, off_one)
    schur = diag_two - jnp.dot(lower_coupling, lower_coupling.T, precision=highest)
    chol_two = jnp.linalg.cholesky(schur)
    shifted = off_two - jnp.dot(lower_one, lower_coupling.T, precision=highest)
    lower_two = right_solve(chol_two, shifted)
    blocks_one = lower_one.reshape(NBLK, BLK, W)
    blocks_two = lower_two.reshape(NBLK, BLK, W)
    groups = KTOT // 16
    row_ids = pattern[:, 0].astype(jnp.int32).reshape(groups, 16)
    col_ids = pattern[:, 1].astype(jnp.int32).reshape(groups, 16)
    tiles = targets.reshape(groups, 16, BLK, BLK)

    def one_group(items):
        tile, row_id, col_id = items
        first = jnp.einsum('kaw,kbw->kab', blocks_one[row_id], blocks_one[col_id], precision=highest)
        second = jnp.einsum('kaw,kbw->kab', blocks_two[row_id], blocks_two[col_id], precision=highest)
        return tile - (first + second)
    updated = lax.map(one_group, (tiles, row_ids, col_ids)).reshape(KTOT, BLK, BLK)
    return (lower_one, lower_two, updated)
```

```python
import functools

import jax
import jax.numpy as jnp
from jax import lax
from jax.experimental import pallas as pl
from jax.experimental.pallas import tpu as pltpu
from jax.sharding import PartitionSpec as P


HIGHEST = lax.Precision.HIGHEST
F32 = jnp.float32
BF16 = jnp.bfloat16
BLK = 128
W = 512
NB = 32


def dot(a, b, ca, cb, precision=HIGHEST):
    return lax.dot_general(
        a, b, (((ca,), (cb,)), ((), ())), precision=precision, preferred_element_type=F32
    )


def split(x):
    high = x.astype(BF16)
    return high, (x - high.astype(F32)).astype(BF16)


def dot_split(a_high, a_low, b_high, b_low, ca, cb):
    one = functools.partial(dot, ca=ca, cb=cb, precision=None)
    return one(a_high, b_high) + one(a_low, b_high) + one(a_high, b_low)


def base_factor(w_ref, first):
    row = lax.broadcasted_iota(jnp.int32, (8, 128), 0)
    tiles = NB // 8

    def part(tile, lanes):
        return w_ref[first + 8 * tile : first + 8 * tile + 8, lanes]

    cols = [
        [
            jnp.broadcast_to(part(t, slice(first + j, first + j + 1)), (8, 128))
            if t >= j // 8
            else None
            for t in range(tiles)
        ]
        for j in range(NB)
    ]
    rows = [[part(t, slice(0, 128)), part(t, slice(128, 256))] for t in range(tiles)]
    pivots = [jnp.zeros((8, 128), F32) for _ in range(tiles)]
    for k in range(NB):
        at, sub = k // 8, k % 8
        pivot = jnp.broadcast_to(cols[k][at][sub : sub + 1, :], (8, 128))
        pivots[at] = jnp.where(row == sub, pivot, pivots[at])
        if k == NB - 1:
            break
        inverse = 1.0 / pivot
        factors = [cols[k][t] * inverse if t >= at else None for t in range(tiles)]
        factors[at] = jnp.where(row > sub, factors[at], 0.0)
        for j in range(k + 1, NB):
            other = jnp.broadcast_to(cols[k][j // 8][j % 8 : j % 8 + 1, :], (8, 128))
            for t in range(j // 8, tiles):
                cols[j][t] = cols[j][t] - factors[t] * other
        for g in range(2):
            other = jnp.broadcast_to(rows[at][g][sub : sub + 1, :], (8, 128))
            for t in range(at, tiles):
                if t == at and sub == 7:
                    continue
                rows[t][g] = rows[t][g] - factors[t] * other
    for t in range(tiles):
        scale = lax.rsqrt(pivots[t])
        scale = scale * (1.5 - 0.5 * pivots[t] * scale * scale)
        for g in range(2):
            w_ref[first + 8 * t : first + 8 * t + 8, g * 128 : g * 128 + 128] = rows[t][g] * scale


def identity(n):
    return (
        lax.broadcasted_iota(jnp.int32, (n, n), 0) == lax.broadcasted_iota(jnp.int32, (n, n), 1)
    ).astype(F32)


def factor(a, inv, w):
    n = a.shape[0]
    inv[...] = identity(n)

    def outer(o, carry):
        ro = pl.multiple_of(o * BLK, BLK)
        w[:, 0:BLK] = a[pl.ds(ro, BLK), pl.ds(ro, BLK)]
        w[:, BLK : 2 * BLK] = identity(BLK)
        for first in range(0, BLK, NB):
            base_factor(w, first)
            end = first + NB
            if end < BLK:
                u = w[first:end, :]
                w[end:BLK, :] = w[end:BLK, :] - dot(w[first:end, 0:BLK], u, 0, 0)[end:BLK, :]
        r = w[:, BLK : 2 * BLK]
        a[pl.ds(ro, BLK), :] = dot(r, a[pl.ds(ro, BLK), :], 1, 0)
        inv[pl.ds(ro, BLK), :] = dot(r, inv[pl.ds(ro, BLK), :], 1, 0)

        def trail(q, carry):
            rq = pl.multiple_of(q * BLK, BLK)
            u = a[pl.ds(ro, BLK), pl.ds(rq, BLK)]
            a[pl.ds(rq, BLK), :] = a[pl.ds(rq, BLK), :] - dot(u, a[pl.ds(ro, BLK), :], 0, 0)
            inv[pl.ds(rq, BLK), :] = inv[pl.ds(rq, BLK), :] - dot(u, inv[pl.ds(ro, BLK), :], 0, 0)
            return carry

        lax.fori_loop(o + 1, n // BLK, trail, 0)
        return carry

    lax.fori_loop(0, n // BLK, outer, 0)


def place(pieces, which, row, col, target):
    x, z, y, core = row // 4, row % 4, col // 2, col % 2

    def one(n, carry):
        dc, dy, dx, dz = n // 64, n // 16 % 4, n // 4 % 4, n % 4
        source = ((x - dx) & 3) * 4 + ((z - dz) & 3)
        at = pl.multiple_of(source * 32 + ((y - dy) & 3) * 8, 8)
        lane = pl.multiple_of(((core + dc) & 1) * 256, 256)
        target[pl.ds(at, 8), pl.ds(lane, 256)] = pieces[n, which]
        return carry

    lax.fori_loop(0, 128, one, 0)


def first_kernel(place_ref, pieces, inv_ref, a, w):
    place(pieces, 0, place_ref[0], place_ref[1], a)
    factor(a, inv_ref, w)


def second_kernel(place_ref, pieces, inv_one, out_ref, a, c, inv, w):
    row, col = place_ref[0], place_ref[1]
    place(pieces, 0, row, col, c)
    place(pieces, 1, row, col, a)
    n = a.shape[0]

    def couple(q, carry):
        rows = pl.ds(pl.multiple_of(q * BLK, BLK), BLK)
        c[rows, :] = dot(c[rows, :], inv_one[...], 1, 1)
        return carry

    lax.fori_loop(0, n // BLK, couple, 0)

    def schur(q, carry):
        rows = pl.ds(pl.multiple_of(q * BLK, BLK), BLK)
        a[rows, :] = a[rows, :] - dot(c[rows, :], c[...], 1, 1)
        return carry

    lax.fori_loop(0, n // BLK, schur, 0)
    def chain(q, carry):
        rows = pl.ds(pl.multiple_of(q * BLK, BLK), BLK)
        c[rows, :] = dot(c[rows, :], inv_one[...], 1, 0)
        return carry

    lax.fori_loop(0, n // BLK, chain, 0)
    factor(a, inv, w)
    out_ref[0:n, 0:n] = inv_one[...]
    out_ref[0:n, n : 2 * n] = jnp.zeros((n, n), F32)
    out_ref[n : 2 * n, n : 2 * n] = inv[...]

    def corner(q, carry):
        rows = pl.multiple_of(q * BLK, BLK)
        out_ref[pl.ds(n + rows, BLK), 0:n] = -dot(inv[pl.ds(rows, BLK), :], c[...], 1, 0)
        return carry

    lax.fori_loop(0, n // BLK, corner, 0)


VM = pl.BlockSpec(memory_space=pltpu.VMEM)
SM = pl.BlockSpec(memory_space=pltpu.SMEM)
ANY = pl.BlockSpec(memory_space=pl.ANY)


def first_factor(where, pieces):
    return pl.pallas_call(
        first_kernel,
        out_shape=jax.ShapeDtypeStruct((W, W), F32),
        in_specs=[SM, VM],
        out_specs=VM,
        scratch_shapes=[pltpu.VMEM((W, W), F32), pltpu.VMEM((BLK, 2 * BLK), F32)],
        cost_estimate=pl.CostEstimate(flops=10**9, bytes_accessed=80 * 10**6, transcendentals=0),
        name="first_factor",
    )(where, pieces)


def second_factor(where, pieces, inv_one):
    return pl.pallas_call(
        second_kernel,
        out_shape=jax.ShapeDtypeStruct((2 * W, 2 * W), F32),
        in_specs=[SM, VM, VM],
        out_specs=VM,
        scratch_shapes=[
            pltpu.VMEM((W, W), F32),
            pltpu.VMEM((W, W), F32),
            pltpu.VMEM((W, W), F32),
            pltpu.VMEM((BLK, 2 * BLK), F32),
        ],
        cost_estimate=pl.CostEstimate(flops=10**9, bytes_accessed=100 * 10**6, transcendentals=0),
        name="second_factor",
    )(where, pieces, inv_one)


def panel_kernel(one_ref, two_ref, inv_ref, lower_one, lower_two, amat_high, amat_low, ih, il):
    n = inv_ref.shape[0]

    def halves(q, carry):
        rows = pl.ds(pl.multiple_of(q * BLK, BLK), BLK)
        ih[rows, :], il[rows, :] = split(inv_ref[rows, :])
        return carry

    lax.fori_loop(0, n // BLK, halves, 0)
    oh, ol = split(one_ref[...])
    th, tl = split(two_ref[...])
    for g in range(2):
        half = slice(g * 256, g * 256 + 256)
        lower_one[:, half] = dot_split(oh, ol, ih[half, 0:W], il[half, 0:W], 1, 1)
        rest = slice(W + g * 256, W + g * 256 + 256)
        lower_two[:, half] = dot_split(
            oh, ol, ih[rest, 0:W], il[rest, 0:W], 1, 1
        ) + dot_split(th, tl, ih[rest, W:], il[rest, W:], 1, 1)

    def amat(q, carry):
        cols = pl.ds(pl.multiple_of(q * 256, 256), 256)
        for g in range(4):
            lanes = slice(g * 256, g * 256 + 256)
            value = dot_split(ih[:, cols], il[:, cols], ih[:, lanes], il[:, lanes], 0, 0)
            amat_high[cols, lanes], amat_low[cols, lanes] = split(value)
        return carry

    lax.fori_loop(0, n // 256, amat, 0)


def panels(one, two, inv):
    n = inv.shape[0]
    return pl.pallas_call(
        panel_kernel,
        out_shape=[jax.ShapeDtypeStruct(one.shape, F32)] * 2
        + [jax.ShapeDtypeStruct((n, n), BF16)] * 2,
        in_specs=[VM] * 3,
        out_specs=[VM] * 4,
        scratch_shapes=[pltpu.VMEM((n, n), BF16)] * 2,
        cost_estimate=pl.CostEstimate(flops=8 * 10**9, bytes_accessed=16 * 10**6, transcendentals=0),
        name="panels",
    )(one, two, inv)


def rows_kernel(*refs):
    pieces = refs[:8]
    amat_high, amat_low, y_high, y_low, held, sems = refs[8:]
    n = amat_high.shape[0]
    size = pieces[0].shape[0]
    copies = [
        pltpu.make_async_copy(pieces[p], held.at[pl.ds(p * size, size), :], sems.at[p])
        for p in range(8)
    ]
    for copy in copies:
        copy.start()
    for copy in copies:
        copy.wait()

    def body(q, carry):
        rows = pl.ds(pl.multiple_of(q * 256, 256), 256)
        xh, xl = split(held[rows, :])
        for g in range(n // 256):
            lanes = slice(g * 256, g * 256 + 256)
            value = dot_split(xh, xl, amat_high[:, lanes], amat_low[:, lanes], 1, 0)
            y_high[rows, lanes], y_low[rows, lanes] = split(value)
        return carry

    lax.fori_loop(0, 8 * size // 256, body, 0)


def row_side(pieces, amat_high, amat_low):
    size, n = pieces[0].shape
    return pl.pallas_call(
        rows_kernel,
        out_shape=[jax.ShapeDtypeStruct((8 * size, n), BF16)] * 2,
        in_specs=[ANY] * 8 + [VM] * 2,
        out_specs=[VM] * 2,
        scratch_shapes=[pltpu.VMEM((8 * size, n), F32), pltpu.SemaphoreType.DMA((8,))],
        compiler_params=pltpu.CompilerParams(vmem_limit_bytes=40 << 20),
        cost_estimate=pl.CostEstimate(flops=13 * 10**9, bytes_accessed=30 * 10**6, transcendentals=0),
        name="row_side",
    )(*pieces, amat_high, amat_low)


def update_kernel(
    place_ref, pattern, y_high, y_low, cols_ref, targets, updated,
    count, by_row, pair_a, pair_b, xh, xl, stage, tv, stage_sems, sems,
):
    blocks = targets.shape[0]
    col = place_ref[1]
    load = pltpu.make_async_copy(targets, tv, sems.at[0])
    load.start()
    pieces = cols_ref.shape[0] // 256

    def fetch(p, slot):
        return pltpu.make_async_copy(
            cols_ref.at[pl.ds(pl.multiple_of(p * 256, 256), 256), :], stage.at[slot], stage_sems.at[slot]
        )

    depth = stage.shape[0]
    for p in range(depth - 1):
        fetch(p, p).start()

    for i in range(16):
        count[i] = 0

    def sort(k, carry):
        i = pattern[2 * k] & 15
        seen = count[i]
        by_row[i * blocks + seen] = k
        count[i] = seen + 1
        return carry

    lax.fori_loop(0, blocks, sort, 0)

    def pair_row(i, total):
        n = count[i]

        def one(q, carry):
            pair_a[total + q] = by_row[i * blocks + 2 * q]
            pair_b[total + q] = by_row[i * blocks + jnp.minimum(2 * q + 1, n - 1)]
            return carry

        half = (n + 1) // 2
        lax.fori_loop(0, half, one, 0)
        return total + half

    pairs = lax.fori_loop(0, 16, pair_row, 0)

    def take(p, carry):
        slot = lax.rem(p, depth)
        fetch(p, slot).wait()

        @pl.when(p + depth - 1 < pieces)
        def _():
            fetch(p + depth - 1, lax.rem(p + depth - 1, depth)).start()

        rows = pl.ds(pl.multiple_of(p * 256, 256), 256)
        xh[rows, :], xl[rows, :] = split(stage[slot])
        return carry

    lax.fori_loop(0, pieces, take, 0)
    load.wait()

    def column(k):
        j = pattern[2 * k + 1]
        return pl.ds(pl.multiple_of((j // 16 * 2 + (j & 1)) * BLK, BLK), BLK)

    def step(q, carry):
        a, b = pair_a[q], pair_b[q]
        i = pattern[2 * a] & 15
        dy = (col // 2 - i // 4) & 3
        dc = (col + i // 2) & 1
        rows = pl.ds(pl.multiple_of(((dc * 4 + dy) * 2 + (i & 1)) * BLK, BLK), BLK)
        ja, jb = column(a), column(b)
        high = jnp.concatenate([xh[ja, :], xh[jb, :]], axis=0)
        low = jnp.concatenate([xl[ja, :], xl[jb, :]], axis=0)
        value = dot_split(y_high[rows, :], y_low[rows, :], high, low, 1, 1)
        tv[a] = tv[a] - value[:, 0:BLK]
        pltpu.make_async_copy(tv.at[a], updated.at[a], sems.at[1]).start()

        @pl.when(a != b)
        def _():
            tv[b] = tv[b] - value[:, BLK : 2 * BLK]
            pltpu.make_async_copy(tv.at[b], updated.at[b], sems.at[1]).start()

        return carry

    lax.fori_loop(0, pairs, step, 0)
    pltpu.make_async_copy(tv, updated, sems.at[1]).wait()


def updates(where, pattern, y_high, y_low, cols, targets):
    blocks = targets.shape[0]
    return pl.pallas_call(
        update_kernel,
        out_shape=jax.ShapeDtypeStruct(targets.shape, F32),
        in_specs=[SM, SM, VM, VM, ANY, ANY],
        out_specs=ANY,
        scratch_shapes=[
            pltpu.SMEM((16,), jnp.int32),
            pltpu.SMEM((16 * blocks,), jnp.int32),
            pltpu.SMEM((blocks,), jnp.int32),
            pltpu.SMEM((blocks,), jnp.int32),
            pltpu.VMEM(cols.shape, BF16),
            pltpu.VMEM(cols.shape, BF16),
            pltpu.VMEM((4, 256, cols.shape[1]), F32),
            pltpu.VMEM(targets.shape, F32),
            pltpu.SemaphoreType.DMA((4,)),
            pltpu.SemaphoreType.DMA((2,)),
        ],
        compiler_params=pltpu.CompilerParams(vmem_limit_bytes=48 << 20),
        cost_estimate=pl.CostEstimate(flops=13 * 10**9, bytes_accessed=40 * 10**6, transcendentals=0),
        name="updates",
    )(where, pattern, y_high, y_low, cols, targets)


ALONG_Z = ("row", lambda s: [(x * 4 + z, x * 4 + (z + s) % 4) for x in range(4) for z in range(4)])
ALONG_X = ("row", lambda s: [(x * 4 + z, (x + s) % 4 * 4 + z) for x in range(4) for z in range(4)])
ALONG_Y = ("col", lambda s: [(y * 2 + c, (y + s) % 4 * 2 + c) for y in range(4) for c in range(2)])
SWAP = [(c, c ^ 1) for c in range(8)]


def ring(x, along):
    axis, shift = along
    return [x] + [lax.ppermute(x, axis, shift(s)) for s in (1, 2, 3)]


def spread(x):
    x = x[None]
    for along in (ALONG_Z, ALONG_X, ALONG_Y):
        x = jnp.concatenate(ring(x, along), axis=0)
    return jnp.concatenate([x, lax.ppermute(x, "col", SWAP)], axis=0)


def shards(diag_one, coupling, diag_two, off_one, off_two, targets, pattern):
    row, col = lax.axis_index("row"), lax.axis_index("col")
    where = jnp.stack([row, col]).astype(jnp.int32)
    y, core = col // 2, col % 2

    def own(x):
        return lax.dynamic_slice(x, (y * 8, core * 256), (8, 256))

    pieces_one = spread(own(diag_one)[None])
    pieces_two = spread(jnp.stack([own(coupling), own(diag_two)]))
    both = jnp.concatenate([off_one, off_two], axis=1)
    cols = lax.all_gather(both, "row", axis=0, tiled=True)
    near = ring(both, ALONG_Y)
    rows = near + [lax.ppermute(x, "col", SWAP) for x in near]
    inv_one = first_factor(where, pieces_one)
    inv = second_factor(where, pieces_two, inv_one)
    lower_one, lower_two, amat_high, amat_low = panels(off_one, off_two, inv)
    y_high, y_low = row_side(rows, amat_high, amat_low)
    updated = updates(where, pattern.reshape(-1), y_high, y_low, cols, targets)
    return (lower_one, lower_two, updated)


def solution(mesh):
    return jax.shard_map(
        shards,
        mesh=mesh,
        in_specs=(
            P("row", None),
            P("row", None),
            P("row", None),
            P(("row", "col"), None),
            P(("row", "col"), None),
            P(("row", "col"), None, None),
            P(("row", "col"), None),
        ),
        out_specs=(P(("row", "col"), None), P(("row", "col"), None), P(("row", "col"), None, None)),
        check_vma=False,
    )
```

```python
import functools

import jax
import jax.numpy as jnp
from jax import lax
from jax.experimental import pallas as pl
from jax.experimental.pallas import tpu as pltpu
from jax.sharding import PartitionSpec as P


HIGHEST = lax.Precision.HIGHEST
F32 = jnp.float32
BF16 = jnp.bfloat16
BLK = 128
W = 512
NB = 32


def dot(a, b, ca, cb, precision=HIGHEST):
    return lax.dot_general(
        a, b, (((ca,), (cb,)), ((), ())), precision=precision, preferred_element_type=F32
    )


def split(x):
    high = x.astype(BF16)
    return high, (x - high.astype(F32)).astype(BF16)


def dot_split(a_high, a_low, b_high, b_low, ca, cb):
    one = functools.partial(dot, ca=ca, cb=cb, precision=None)
    return one(a_high, b_high) + one(a_low, b_high) + one(a_high, b_low)


def base_factor(w_ref, first):
    row = lax.broadcasted_iota(jnp.int32, (8, 128), 0)
    tiles = NB // 8

    def part(tile, lanes):
        return w_ref[first + 8 * tile : first + 8 * tile + 8, lanes]

    cols = [
        [
            jnp.broadcast_to(part(t, slice(first + j, first + j + 1)), (8, 128))
            if t >= j // 8
            else None
            for t in range(tiles)
        ]
        for j in range(NB)
    ]
    rows = [[part(t, slice(0, 128)), part(t, slice(128, 256))] for t in range(tiles)]
    pivots = [jnp.zeros((8, 128), F32) for _ in range(tiles)]
    for k in range(NB):
        at, sub = k // 8, k % 8
        pivot = jnp.broadcast_to(cols[k][at][sub : sub + 1, :], (8, 128))
        pivots[at] = jnp.where(row == sub, pivot, pivots[at])
        if k == NB - 1:
            break
        inverse = 1.0 / pivot
        factors = [cols[k][t] * inverse if t >= at else None for t in range(tiles)]
        factors[at] = jnp.where(row > sub, factors[at], 0.0)
        for j in range(k + 1, NB):
            other = jnp.broadcast_to(cols[k][j // 8][j % 8 : j % 8 + 1, :], (8, 128))
            for t in range(j // 8, tiles):
                cols[j][t] = cols[j][t] - factors[t] * other
        for g in range(2):
            other = jnp.broadcast_to(rows[at][g][sub : sub + 1, :], (8, 128))
            for t in range(at, tiles):
                if t == at and sub == 7:
                    continue
                rows[t][g] = rows[t][g] - factors[t] * other
    for t in range(tiles):
        scale = lax.rsqrt(pivots[t])
        scale = scale * (1.5 - 0.5 * pivots[t] * scale * scale)
        for g in range(2):
            w_ref[first + 8 * t : first + 8 * t + 8, g * 128 : g * 128 + 128] = rows[t][g] * scale


def identity(n):
    return (
        lax.broadcasted_iota(jnp.int32, (n, n), 0) == lax.broadcasted_iota(jnp.int32, (n, n), 1)
    ).astype(F32)


def factor(a, inv, w):
    n = a.shape[0]
    inv[...] = identity(n)

    def outer(o, carry):
        ro = pl.multiple_of(o * BLK, BLK)
        w[:, 0:BLK] = a[pl.ds(ro, BLK), pl.ds(ro, BLK)]
        w[:, BLK : 2 * BLK] = identity(BLK)
        for first in range(0, BLK, NB):
            base_factor(w, first)
            end = first + NB
            if end < BLK:
                u = w[first:end, :]
                w[end:BLK, :] = w[end:BLK, :] - dot(w[first:end, 0:BLK], u, 0, 0)[end:BLK, :]
        r = w[:, BLK : 2 * BLK]
        a[pl.ds(ro, BLK), :] = dot(r, a[pl.ds(ro, BLK), :], 1, 0)
        inv[pl.ds(ro, BLK), :] = dot(r, inv[pl.ds(ro, BLK), :], 1, 0)

        def trail(q, carry):
            rq = pl.multiple_of(q * BLK, BLK)
            u = a[pl.ds(ro, BLK), pl.ds(rq, BLK)]
            a[pl.ds(rq, BLK), :] = a[pl.ds(rq, BLK), :] - dot(u, a[pl.ds(ro, BLK), :], 0, 0)
            inv[pl.ds(rq, BLK), :] = inv[pl.ds(rq, BLK), :] - dot(u, inv[pl.ds(ro, BLK), :], 0, 0)
            return carry

        lax.fori_loop(o + 1, n // BLK, trail, 0)
        return carry

    lax.fori_loop(0, n // BLK, outer, 0)


def place(mine, other, which, col, target):
    rows = mine.shape[2]

    def one(n, carry):
        at = pl.ds(pl.multiple_of(n * rows, rows), rows)
        lane = (col & 1) * 256
        target[at, pl.ds(pl.multiple_of(lane, 256), 256)] = mine[n, which]
        target[at, pl.ds(pl.multiple_of(256 - lane, 256), 256)] = other[n, which]
        return carry

    lax.fori_loop(0, mine.shape[0], one, 0)


def first_kernel(place_ref, pairs, mine, other, inv_ref, a, w):
    place(mine, other, 0, place_ref[1], a)
    factor(a, inv_ref, w)


def second_kernel(place_ref, mine, other, inv_one, out_ref, a, c, inv, w, ih, il, ch, cl):
    n = a.shape[0]
    half = n // 2
    place(mine, other, 1, place_ref[1], c)
    place(mine, other, 2, place_ref[1], a)
    ih[...], il[...] = split(inv_one[...])
    ch[...], cl[...] = split(c[...])
    for g in range(2):
        lanes = slice(g * half, g * half + half)
        k = slice(0, g * half + half)
        c[:, lanes] = dot_split(ch[:, k], cl[:, k], ih[lanes, k], il[lanes, k], 1, 1)
    ch[...], cl[...] = split(c[...])
    for g in range(2):
        lanes = slice(g * half, g * half + half)
        a[:, lanes] = a[:, lanes] - dot_split(ch[...], cl[...], ch[lanes, :], cl[lanes, :], 1, 1)
    for g in range(2):
        lanes = slice(g * half, g * half + half)
        k = slice(g * half, n)
        c[:, lanes] = dot_split(ch[:, k], cl[:, k], ih[k, lanes], il[k, lanes], 1, 0)
    ch[...], cl[...] = split(c[...])
    factor(a, inv, w)
    ih[...], il[...] = split(inv[...])
    out_ref[0:n, 0:n] = inv_one[...]
    out_ref[0:n, n : 2 * n] = jnp.zeros((n, n), F32)
    out_ref[n : 2 * n, n : 2 * n] = inv[...]
    for g in range(2):
        rows = slice(g * half, g * half + half)
        k = slice(0, g * half + half)
        out_ref[n + g * half : n + g * half + half, 0:n] = -dot_split(
            ih[rows, k], il[rows, k], ch[k, :], cl[k, :], 1, 0
        )


VM = pl.BlockSpec(memory_space=pltpu.VMEM)
SM = pl.BlockSpec(memory_space=pltpu.SMEM)
ANY = pl.BlockSpec(memory_space=pl.ANY)


def first_factor(where, pairs, mine, other):
    return pl.pallas_call(
        first_kernel,
        out_shape=jax.ShapeDtypeStruct((W, W), F32),
        in_specs=[SM, SM, VM, VM],
        out_specs=VM,
        scratch_shapes=[pltpu.VMEM((W, W), F32), pltpu.VMEM((BLK, 2 * BLK), F32)],
        cost_estimate=pl.CostEstimate(flops=10**9, bytes_accessed=80 * 10**6, transcendentals=0),
        name="first_factor",
    )(where, pairs, mine, other)


def second_factor(where, mine, other, inv_one):
    return pl.pallas_call(
        second_kernel,
        out_shape=jax.ShapeDtypeStruct((2 * W, 2 * W), F32),
        in_specs=[SM, VM, VM, VM],
        out_specs=VM,
        scratch_shapes=[
            pltpu.VMEM((W, W), F32),
            pltpu.VMEM((W, W), F32),
            pltpu.VMEM((W, W), F32),
            pltpu.VMEM((BLK, 2 * BLK), F32),
        ]
        + [pltpu.VMEM((W, W), BF16)] * 4,
        cost_estimate=pl.CostEstimate(flops=10**9, bytes_accessed=100 * 10**6, transcendentals=0),
        name="second_factor",
    )(where, mine, other, inv_one)


ROWS = 1024


def rows_kernel(*refs):
    pieces, inv_ref = refs[:8], refs[8]
    lower_one, lower_two, y_high, y_low = refs[9:13]
    ih, il, xh, xl, lh, ll, held, sems = refs[13:]
    n = inv_ref.shape[0]
    size = pieces[0].shape[0]
    copies = [
        pltpu.make_async_copy(pieces[p], held.at[pl.ds(p * size, size), :], sems.at[p])
        for p in range(8)
    ]
    for copy in copies:
        copy.start()

    def halves(q, carry):
        rows = pl.ds(pl.multiple_of(q * BLK, BLK), BLK)
        ih[rows, :], il[rows, :] = split(inv_ref[rows, :])
        return carry

    lax.fori_loop(0, n // BLK, halves, 0)
    for copy in copies:
        copy.wait()
    step = 256
    many = lh.shape[0]
    xh[0:size, :], xl[0:size, :] = split(held[0:size, :])
    own = slice(0, size)
    for g in range(n // step):
        lanes, k = slice(g * step, g * step + step), slice(0, g * step + step)
        value = dot_split(xh[own, k], xl[own, k], ih[lanes, k], il[lanes, k], 1, 1)
        out = lower_one if g * step < W else lower_two
        out[:, g * step % W : g * step % W + step] = value

    def body(q, carry):
        rows = pl.ds(pl.multiple_of(q * many, many), many)
        for g in range(n // step):
            lanes = slice(g * step, g * step + step)
            xh[:, lanes], xl[:, lanes] = split(held[rows, lanes])
        for g in range(n // step):
            lanes, k = slice(g * step, g * step + step), slice(0, g * step + step)
            value = dot_split(xh[:, k], xl[:, k], ih[lanes, k], il[lanes, k], 1, 1)
            lh[:, lanes], ll[:, lanes] = split(value)
        for g in range(n // step):
            lanes, k = slice(g * step, g * step + step), slice(g * step, n)
            value = dot_split(lh[:, k], ll[:, k], ih[k, lanes], il[k, lanes], 1, 0)
            y_high[rows, lanes], y_low[rows, lanes] = split(value)
        return carry

    lax.fori_loop(0, 8 * size // many, body, 0)


def row_side(pieces, inv):
    size, n = pieces[0].shape
    return pl.pallas_call(
        rows_kernel,
        out_shape=[jax.ShapeDtypeStruct((size, W), F32)] * 2
        + [jax.ShapeDtypeStruct((8 * size, n), BF16)] * 2,
        in_specs=[ANY] * 8 + [VM],
        out_specs=[VM] * 4,
        scratch_shapes=[pltpu.VMEM((n, n), BF16)] * 2
        + [pltpu.VMEM((ROWS, n), BF16)] * 4
        + [pltpu.VMEM((8 * size, n), F32), pltpu.SemaphoreType.DMA((8,))],
        compiler_params=pltpu.CompilerParams(vmem_limit_bytes=40 << 20),
        cost_estimate=pl.CostEstimate(flops=16 * 10**9, bytes_accessed=30 * 10**6, transcendentals=0),
        name="row_side",
    )(*pieces, inv)


UNROLL = 4


def plan_kernel(pattern, pairs, count, by_row):
    blocks = pattern.shape[0] // 2
    for i in range(16):
        count[i] = 0

    def sort(k, carry):
        i = pattern[2 * k] & 15
        seen = count[i]
        by_row[i * blocks + seen] = k
        count[i] = seen + 1
        return carry

    lax.fori_loop(0, blocks, sort, 0)

    def pair_row(i, total):
        n = count[i]
        half = (n + 1) // 2

        def one(q, carry):
            k = by_row[i * blocks + jnp.minimum(q, n - 1)]
            pairs[2 * total + q] = jnp.where(q < n, k, -1 - k)
            return carry

        lax.fori_loop(0, 2 * half, one, 0)
        return total + half

    total = lax.fori_loop(0, 16, pair_row, 0)
    for q in range(2 * (UNROLL - 1)):
        pairs[2 * total + q] = -1
    pairs[pairs.shape[0] - 1] = (total + UNROLL - 1) // UNROLL


def plan(pattern):
    blocks = pattern.shape[0] // 2
    return pl.pallas_call(
        plan_kernel,
        out_shape=jax.ShapeDtypeStruct((blocks + 16 + 2 * UNROLL + 1,), jnp.int32),
        in_specs=[SM],
        out_specs=SM,
        scratch_shapes=[pltpu.SMEM((16,), jnp.int32), pltpu.SMEM((16 * blocks,), jnp.int32)],
        name="plan",
    )(pattern)


def update_kernel(
    place_ref, pattern, pairs, y_high, y_low, cols_ref, targets, updated,
    xh, xl, stage, tv, stage_sems, sems,
):
    blocks = targets.shape[0]
    col = place_ref[1]
    pieces = stage.shape[0] // 256

    def fetch(p):
        rows = pl.ds(pl.multiple_of(p * 256, 256), 256)
        return pltpu.make_async_copy(cols_ref.at[rows, :], stage.at[rows, :], stage_sems.at[p])

    for p in range(pieces):
        fetch(p).start()
    load = pltpu.make_async_copy(targets, tv.at[pl.ds(0, blocks)], sems.at[0])
    load.start()

    def take(p, carry):
        fetch(p).wait()
        rows = pl.ds(pl.multiple_of(p * 256, 256), 256)
        xh[rows, :], xl[rows, :] = split(stage[rows, :])
        return carry

    lax.fori_loop(0, pieces, take, 0)
    load.wait()

    def column(k):
        j = pattern[2 * k + 1]
        return pl.ds(pl.multiple_of((j // 16 * 2 + (j & 1)) * BLK, BLK), BLK)

    def step(q, carry):
        listed = [pairs[2 * UNROLL * q + n] for n in range(2 * UNROLL)]
        for u in range(UNROLL):
            two = listed[2 * u : 2 * u + 2]
            ks = [jnp.where(k < 0, -1 - k, k) for k in two]
            i = pattern[2 * ks[0]] & 15
            dy = (col // 2 - i // 4) & 3
            dc = (col + i // 2) & 1
            rows = pl.ds(pl.multiple_of(((dc * 4 + dy) * 2 + (i & 1)) * BLK, BLK), BLK)
            ja, jb = column(ks[0]), column(ks[1])
            high = jnp.concatenate([xh[ja, :], xh[jb, :]], axis=0)
            low = jnp.concatenate([xl[ja, :], xl[jb, :]], axis=0)
            y = jnp.concatenate([y_high[rows, :], y_low[rows, :]], axis=0)
            value = dot(y, high, 1, 1, None)
            value = value[0:BLK] + value[BLK:] + dot(y_high[rows, :], low, 1, 1, None)
            for g in range(2):
                at = jnp.where(two[g] < 0, blocks, two[g])
                tv[at] = tv[at] - value[:, g * BLK : g * BLK + BLK]
        for k in listed:

            @pl.when(k >= 0)
            def _():
                pltpu.make_async_copy(tv.at[k], updated.at[k], sems.at[1]).start()

        return carry

    lax.fori_loop(0, pairs[pairs.shape[0] - 1], step, 0)
    pltpu.make_async_copy(tv.at[pl.ds(0, blocks)], updated, sems.at[1]).wait()


def updates(where, pattern, pairs, y_high, y_low, cols, targets):
    blocks = targets.shape[0]
    return pl.pallas_call(
        update_kernel,
        out_shape=jax.ShapeDtypeStruct(targets.shape, F32),
        in_specs=[SM, SM, SM, VM, VM, ANY, ANY],
        out_specs=ANY,
        scratch_shapes=[
            pltpu.VMEM(cols.shape, BF16),
            pltpu.VMEM(cols.shape, BF16),
            pltpu.VMEM(cols.shape, F32),
            pltpu.VMEM((blocks + 1, BLK, BLK), F32),
            pltpu.SemaphoreType.DMA((cols.shape[0] // 256,)),
            pltpu.SemaphoreType.DMA((2,)),
        ],
        compiler_params=pltpu.CompilerParams(vmem_limit_bytes=56 << 20),
        cost_estimate=pl.CostEstimate(flops=13 * 10**9, bytes_accessed=40 * 10**6, transcendentals=0),
        name="updates",
    )(where, pattern, pairs, y_high, y_low, cols, targets)


ALONG_Y = ("col", lambda s: [(y * 2 + c, (y + s) % 4 * 2 + c) for y in range(4) for c in range(2)])
SWAP = [(c, c ^ 1) for c in range(8)]


def ring(x, along):
    axis, shift = along
    return [x] + [lax.ppermute(x, axis, shift(s)) for s in (1, 2, 3)]


def spread(x):
    n = lax.axis_size("row")
    x = lax.all_to_all(jnp.broadcast_to(x[None], (n,) + x.shape), "row", 0, 0, tiled=True)
    return x, lax.ppermute(x, "col", SWAP)


def work(diag_one, coupling, diag_two, off_one, off_two, targets, pattern):
    row, col = lax.axis_index("row"), lax.axis_index("col")
    where = jnp.stack([row, col]).astype(jnp.int32)

    def own(x):
        return lax.dynamic_slice(x, (0, (col & 1) * 256), (x.shape[0], 256))

    mine, other = spread(jnp.stack([own(diag_one), own(coupling), own(diag_two)]))
    both = jnp.concatenate([off_one, off_two], axis=1)
    cols = lax.all_gather(both, "row", axis=0, tiled=True)
    near = ring(both, ALONG_Y)
    pattern = pattern.reshape(-1)
    pairs = plan(pattern)
    inv_one = first_factor(where, pairs, mine, other)
    near, inv_one = lax.optimization_barrier((near, inv_one))
    rows = near + [lax.ppermute(x, "col", SWAP) for x in near]
    inv = second_factor(where, mine, other, inv_one)
    lower_one, lower_two, y_high, y_low = row_side(rows, inv)
    updated = updates(where, pattern, pairs, y_high, y_low, cols, targets)
    return (lower_one, lower_two, updated)


def solution(mesh):
    return jax.shard_map(
        work,
        mesh=mesh,
        in_specs=(
            P("row", None),
            P("row", None),
            P("row", None),
            P(("row", "col"), None),
            P(("row", "col"), None),
            P(("row", "col"), None, None),
            P(("row", "col"), None),
        ),
        out_specs=(P(("row", "col"), None), P(("row", "col"), None), P(("row", "col"), None, None)),
        check_vma=False,
    )
```
